32 devices in a mesh: row: 8 (over z, y), col: 4 (over x, core).
Axes of the slice: x: 2, y: 2, z: 4, core: 2. Of those that a mesh axis runs over, the one named last changes fastest.
Arguments:
- trailing: float32 [16384, 16384], P('row', 'col'), may hold values from -40 to 40, as said below
- factor_one: float32 [16384, 512], P(('row', 'col')), may hold values from -0.0390625 to 0.0390625
- inverse_one: float32 [512, 512], replicated, may hold values from -1 to 2, as said below
- factor_two_top: float32 [512, 512], replicated, may hold values from -0.0390625 to 0.0390625
- factor_two: float32 [16384, 512], P(('row', 'col')), may hold values from -0.0390625 to 0.0390625
- inverse_two: float32 [512, 512], replicated, may hold values from -1 to 2, as said below
- structure_one: int32 [96], replicated, may hold values from 0 to 127, as said below
- structure_two: int32 [94], replicated, may hold values from 0 to 127, as said below
Outputs:
- column_one: float32 [16384, 512], P(('row', 'col'))
- diagonal_one: float32 [512, 512], replicated
- column_two: float32 [16384, 512], P(('row', 'col'))
- cross_two: float32 [512, 512], replicated
- diagonal_two: float32 [512, 512], replicated
The draws below stay inside these ranges and needn't reach their ends.
Inputs may be any that keep to these rules, and one draw needn't show every extreme that they name: `trailing`: symmetric. `inverse_one`: lower triangular, diagonal between 1 and 2. `inverse_two`: lower triangular, diagonal between 1 and 2. `structure_one`: distinct, rising; lists block 0 and the last block. `structure_two`: distinct, rising, each also listed in structure_one; lists block 0 and the last block.
All inputs are finite; a program needn't handle non-finite values.
Results may differ from the reference program's by a relative error of at most 0.0003.
Values sent between devices are 32-bit elements; how exact they have to be, the bound alone decides.
A program may use at most 128 MiB of HBM per device.

```python
import math
import jax
import jax.numpy as jnp
from jax import lax

W = 512
BLK = 128
M = 16384
SB1 = 96
SB2 = 94


def draw_trailing(key, part):
    normals = jax.random.truncated_normal(jax.random.fold_in(key, 31), -5.0, 5.0, (M, M), jnp.float32)
    symmetric = (normals + normals.T) * 0.7071067811865476
    places = jnp.arange(M, dtype=jnp.int32)
    return symmetric.at[places, places].add(2.0)


def lower_inverse(key):
    diag_values = jax.random.uniform(jax.random.fold_in(key, 1), (W,), jnp.float32, 1.0, 2.0)
    off_diag = jax.random.truncated_normal(jax.random.fold_in(key, 2), -5.0, 5.0, (W, W), jnp.float32) * (0.8 / math.sqrt(W))
    return jnp.tril(off_diag, -1) + jnp.diag(diag_values)


def draw_inverse_one(key, part):
    return lower_inverse(jax.random.fold_in(key, 11))


def draw_inverse_two(key, part):
    return lower_inverse(jax.random.fold_in(key, 12))


def structure_lists(key):
    count = M // BLK
    inner_blocks = jax.random.permutation(jax.random.fold_in(key, 21), count - 2)[:SB1 - 2].astype(jnp.int32) + 1
    ends = jnp.array([0, count - 1], dtype=jnp.int32)
    first_set = jnp.sort(jnp.concatenate([ends, inner_blocks]))
    chosen = jax.random.permutation(jax.random.fold_in(key, 22), SB1 - 2)[:SB2 - 2]
    second_set = jnp.sort(jnp.concatenate([ends, first_set[1:-1][chosen]]))
    return (first_set, second_set)


def draw_structure_one(key, part):
    return structure_lists(key)[0]


def draw_structure_two(key, part):
    return structure_lists(key)[1]


def shard_levels(key, dims, split, smallest, top_value):
    def one(dim, blocks):
        steps = jax.random.uniform(jax.random.fold_in(jax.random.fold_in(key, 6), dim), (blocks,), jnp.float32, smallest / len(split), top_value / len(split))
        return jnp.repeat(jnp.exp(steps), dims[dim] // blocks).reshape((-1,) + (1,) * (len(dims) - dim - 1))

    level = one(*split[0])
    for cut in split[1:]:
        level = level * one(*cut)
    return level


def centred(own_key, shape, deviation, bound, cuts=(), held_as=jnp.bfloat16):
    drawn = jax.random.normal(own_key, shape, jnp.float32) * deviation
    if len(cuts) > 0:
        drawn = shard_levels(own_key, shape, cuts, -0.22, 0.18) * drawn
    return jnp.clip(drawn, min=-bound, max=bound).astype(held_as)


def setup_inputs(seed: int = 0) -> dict:
    splits = jax.random.split(jax.random.key(seed), 9)
    trailing = draw_trailing(jax.random.fold_in(splits[8], 71), 0)
    factor_one = centred(splits[1], (M, W), (2 * SB1 * BLK) ** -0.5, 0.0390625, ((0, 32),), jnp.float32)
    inverse_one = draw_inverse_one(jax.random.fold_in(splits[8], 71), 0)
    factor_two_top = centred(splits[3], (W, W), (2 * (SB2 * BLK + W)) ** -0.5, 0.0390625, (), jnp.float32)
    factor_two = centred(splits[4], (M, W), (2 * (SB2 * BLK + W)) ** -0.5, 0.0390625, ((0, 32),), jnp.float32)
    inverse_two = draw_inverse_two(jax.random.fold_in(splits[8], 71), 0)
    structure_one = draw_structure_one(jax.random.fold_in(splits[8], 71), 0)
    structure_two = draw_structure_two(jax.random.fold_in(splits[8], 71), 0)
    return {"trailing": trailing, "factor_one": factor_one, "inverse_one": inverse_one, "factor_two_top": factor_two_top, "factor_two": factor_two, "inverse_two": inverse_two, "structure_one": structure_one, "structure_two": structure_two}


def product(left, right):
    return jnp.dot(left, right, precision=lax.Precision.HIGHEST, preferred_element_type=jnp.float32)


def block_flags(structure, count):
    blocks = jnp.arange(count, dtype=jnp.int32) // BLK
    hits = jnp.any(blocks[:, None] == structure[None, :].astype(jnp.int32), axis=1)
    return hits.astype(jnp.float32)[:, None]


def reference(trailing, factor_one, inverse_one, factor_two_top, factor_two, inverse_two, structure_one, structure_two):
    mask_one = block_flags(structure_one, M)
    mask_two = block_flags(structure_two, M)
    normal_one = mask_one * product(factor_one, inverse_one)
    column_one = -mask_one * product(trailing, normal_one)
    diagonal_one = product(inverse_one.T, inverse_one) - product(normal_one.T, column_one)
    normal_top = product(factor_two_top, inverse_two)
    normal_two = mask_two * product(factor_two, inverse_two)
    column_two = -mask_two * (product(column_one, normal_top) + product(trailing, normal_two))
    cross_two = -(product(diagonal_one, normal_top) + product(column_one.T, normal_two))
    diagonal_two = product(inverse_two.T, inverse_two) - product(normal_top.T, cross_two) - product(normal_two.T, column_two)
    return column_one, diagonal_one, column_two, cross_two, diagonal_two
```

```python
import jax
import jax.numpy as jnp
from jax import lax
from jax.sharding import PartitionSpec as P

BLK = 128


def product(left, right):
    return jnp.dot(left, right, precision=lax.Precision.HIGHEST, preferred_element_type=jnp.float32)


def big_product(left, right):
    return jnp.dot(left, right, precision=lax.Precision.HIGH, preferred_element_type=jnp.float32)


def block_flags(structure, first_row, count):
    blocks = (first_row + jnp.arange(count, dtype=jnp.int32)) // BLK
    hits = jnp.any(blocks[:, None] == structure[None, :], axis=1)
    return hits.astype(jnp.float32)[:, None]


def column_panel(normal, turn):
    rows, cols = lax.axis_size("row"), lax.axis_size("col")
    if rows == 8 and cols == 4:
        return column_panel_torus(normal, turn)
    moves = [(p, (p % rows) * cols + p // rows) for p in range(rows * cols)]
    piece = lax.ppermute(normal, ("row", "col"), moves)
    return lax.all_gather(piece, "row", axis=0, tiled=True)


def column_panel_torus(normal, turn):
    rows = lax.axis_size("row")
    depth = rows // 2
    moves = []
    for z in range(depth):
        for y in range(2):
            for x in range(2):
                for core in range(2):
                    off = 2 * core + (0 if x == z // 2 else 1)
                    target = (z + off) % depth
                    moves.append(((2 * z + y) * 4 + 2 * x + core, (2 * target + y) * 4 + z))
    across = [(r, r ^ 1) for r in range(rows)]
    up = [(r, (r + 2) % rows) for r in range(rows)]
    down = [(r, (r - 2) % rows) for r in range(rows)]
    half = normal.shape[0] // 2

    def go(x, way):
        return lax.ppermute(x, "row", way)

    a0 = lax.ppermute(normal[:half], ("row", "col"), moves)
    b0 = lax.ppermute(normal[half:], ("row", "col"), moves)
    a1 = go(a0, across)
    b_up, b_down = go(b0, up), go(b0, down)
    a0_up, a0_down = go(a0, up), go(a0, down)
    c0 = go(b0, across)
    a1_up, a1_down = go(a1, up), go(a1, down)
    c_up, c_down = go(b_up, across), go(b_down, across)
    b_far = go(b_up, up) if turn == 0 else go(b_down, down)
    a0_far = go(a0_up, up)
    a1_far = go(a1_down, down)
    c_far = go(b_far, across)

    z, y = lax.axis_index("row") // 2, lax.axis_index("row") % 2
    c = lax.axis_index("col")

    def place(step, other):
        off = (z - step - c) % depth
        x = jnp.where(off % 2 == 0, c // 2, 1 - c // 2)
        return 4 * ((y + other) % 2) + 2 * x + off // 2

    parts = (
        (a0, b0, 0, 0), (a1, c0, 0, 1),
        (a0_up, b_up, 1, 0), (a1_up, c_up, 1, 1),
        (a0_down, b_down, -1, 0), (a1_down, c_down, -1, 1),
        (a0_far, b_far, 2, 0), (a1_far, c_far, 2, 1),
    )
    panel = jnp.zeros((rows * 2 * half, normal.shape[1]), normal.dtype)
    for first, second, step, other in parts:
        at = place(step, other) * (2 * half)
        panel = lax.dynamic_update_slice(panel, first, (at, 0))
        panel = lax.dynamic_update_slice(panel, second, (at + half, 0))
    return lax.optimization_barrier(panel)


def total_over_all(x):
    return lax.psum(x, ("row", "col"))


def sweep(trailing, col_block):
    part = -big_product(trailing, col_block)
    return lax.psum_scatter(part, "col", scatter_dimension=0, tiled=True)


def body(
    trailing,
    factor_one,
    inverse_one,
    factor_two_top,
    factor_two,
    inverse_two,
    structure_one,
    structure_two,
):
    piece_rows = factor_one.shape[0]
    row_index = lax.axis_index("row")
    col_index = lax.axis_index("col")
    first_row = (row_index * lax.axis_size("col") + col_index) * piece_rows
    mask_one = block_flags(structure_one, first_row, piece_rows)
    mask_two = block_flags(structure_two, first_row, piece_rows)
    normal_one = mask_one * product(factor_one, inverse_one)
    cols_one = column_panel(normal_one, 0)
    normal_two = mask_two * product(factor_two, inverse_two)
    cols_two = column_panel(normal_two, 1)
    normal_top = product(factor_two_top, inverse_two)
    summed_one = sweep(trailing, cols_one)
    summed_two = sweep(trailing, cols_two)
    column_one = mask_one * summed_one
    both = product(column_one.T, jnp.concatenate([normal_one, normal_two], axis=1))
    column_two = mask_two * (summed_two - product(column_one, normal_top))
    second = product(normal_two.T, column_two)
    totals = total_over_all(jnp.concatenate([both, second], axis=1))
    width = normal_one.shape[1]
    diagonal_one = product(inverse_one.T, inverse_one) - totals[:, :width].T
    cross_two = -(product(diagonal_one, normal_top) + totals[:, width : 2 * width])
    diagonal_two = (
        product(inverse_two.T, inverse_two)
        - product(normal_top.T, cross_two)
        - totals[:, 2 * width :]
    )
    return (column_one, diagonal_one, column_two, cross_two, diagonal_two)


def solution(mesh):
    return jax.shard_map(
        body,
        mesh=mesh,
        in_specs=(
            P("row", "col"),
            P(("row", "col"), None),
            P(),
            P(),
            P(("row", "col"), None),
            P(),
            P(),
            P(),
        ),
        out_specs=(P(("row", "col"), None), P(), P(("row", "col"), None), P(), P()),
        check_vma=False,
    )
```
